512 devices in a mesh: expert: 128 (over y_hi, z, x), tensor: 4 (over y_lo, core).
Axes of the slice: x: 4, y: 8 (y_hi: 4, y_lo: 2; y = y_hi * 2 + y_lo), z: 8, core: 2. Of those that a mesh axis runs over, the one named last changes fastest.
Arguments:
- tokens: bfloat16 [4096, 4096], P('expert'), may hold values from -6 to 6
- routes: int32 [4096, 8], P('expert'), may hold values from 0 to 127, all different within a row; in each aligned block of 32 rows (0 to 31, 32 to 63, ...) at most 3 rows name the same one
- route_weights: float32 [4096, 8], P('expert'), may hold values from 0.1 to 1
- learner_weights: bfloat16 [128, 4096, 1536], P(None, 'expert', 'tensor'), may hold values from -5 to 5
Outputs:
- combined: bfloat16 [4096, 1536], P('expert', 'tensor')
- expert_amax: float32 [128], P('expert')
The draws below stay inside these ranges and needn't reach their ends.
Inputs may be any that keep to these rules, and one draw needn't show every extreme that they name: `routes`: each row names 8 different experts; within the 32 rows of one index of expert no expert is named by more than 3 rows, a bound that some block reaches there.
All inputs are finite; a program needn't handle non-finite values.
Results may differ from the reference program's by a relative error of at most 0.0049.
Values may be sent and summed in bfloat16 or wider, within the bound.
A program may use at most 64 MiB of HBM per device.

```python
import math
import jax
import jax.numpy as jnp
import numpy as np
from jax import lax

D = 4096
FF = 1536
TOP = 8
TOK_DEV = 32
EXPERTS = 128
CAP = 3
TOKENS = 4096
N_EXPERT = 128


def draw_learner_weights(key, part):
    first_key, second_key, third_key = jax.random.split(key, 3)
    values = jnp.clip(jax.random.normal(first_key, (EXPERTS, D, FF), jnp.float32), -4.5, 4.5)
    row_scale = jnp.exp(jax.random.uniform(second_key, (EXPERTS, D, 1), jnp.float32, -1.15, 1.15))
    column_scale = jnp.exp(jax.random.uniform(third_key, (EXPERTS, 1, FF), jnp.float32, -1.7, 1.7))
    scaled = values * row_scale * column_scale / math.sqrt(2.15 * D)
    return scaled.astype(jnp.bfloat16)


def levels(stream_key, extent, shards, least, high):
    factor_of, own = 1.0, jax.random.fold_in(stream_key, 6)
    for position, parts in shards:
        draws = jnp.exp(jax.random.uniform(jax.random.fold_in(own, position), (parts,), jnp.float32, least / len(shards), high / len(shards)))
        factor_of = factor_of * jnp.repeat(draws, extent[position] // parts).reshape([-1 if axis == position else 1 for axis in range(len(extent))])
    return factor_of


def assign_block(rng, own, number, rows, number_of, top, most, slope):
    ranking = jax.random.permutation(rng, number_of)
    heavy_load, ordinary = load_shares(number_of, rows * top, most, slope, True), load_shares(number_of, rows * top, most, slope, False)
    places = jnp.arange(number_of)

    def named(sizes, offset_by):
        used = int((sizes > 0).sum())
        fixed = max(1, used // 4)
        passed = fixed + (places - fixed + offset_by * (used - fixed)) % max(1, number_of - fixed)
        return jnp.zeros((number_of,), jnp.int32).at[ranking[jnp.where(places < fixed, places, passed)]].set(jnp.asarray(sizes, jnp.int32))

    sizes = jnp.where(number % 4 == 0, named(heavy_load, number // 4), named(ordinary, number - number // 4 - 1))
    mixed = jax.random.permutation(jax.random.fold_in(own, 3), number_of)
    giver, taker = mixed[0:number_of // 2 * 2:2], mixed[1:number_of // 2 * 2:2]
    slack = jnp.minimum(sizes[giver] - 1, most - sizes[taker]) // 2
    slack = jnp.where((giver == ranking[0]) | (taker == ranking[0]) | (sizes[taker] == 0), 0, jnp.maximum(slack, 0))
    passed = jax.random.randint(jax.random.fold_in(own, 4), (number_of // 2,), 0, 1 << 20) % (slack + 1)
    sizes = sizes.at[giver].add(-passed).at[taker].add(passed)
    labels = jnp.searchsorted(jnp.cumsum(sizes), jnp.arange(rows * top), side="right").astype(jnp.int32)
    grid = labels.reshape(top, rows).T
    grid = grid[jax.random.permutation(jax.random.fold_in(own, 1), rows)]
    offset_by = jax.random.randint(jax.random.fold_in(own, 2), (rows, 1), 0, top)
    return jnp.take_along_axis(grid, (jnp.arange(top)[None, :] + offset_by) % top, axis=1)


def load_shares(count, total, reach, skew, full):
    weights = [(1 << 20) // math.isqrt(standing ** skew) + 1 for standing in range(1, count + 1)]
    largest = reach if full else min(reach, max(-(-total // count), total * weights[0] // sum(weights)))
    least = 1 if total - largest >= count - 1 else 0
    counts, spare = [largest] + [least] * (count - 1), total - largest - least * (count - 1)
    while spare > 0:
        movable = [i for i in range(1, count) if counts[i] < largest] or [i for i in range(1, count) if counts[i] < reach]
        pool, remaining = sum([weights[i] for i in movable]), spare
        for i in movable:
            more = min(reach - counts[i], max(1, remaining * weights[i] // pool), spare)
            counts[i] = counts[i] + more
            spare = spare - more
    return np.array(counts)


def scatter_about(stream_key, extent, deviation, most, shards=(), held_as=jnp.bfloat16):
    drawn = deviation * jax.random.normal(stream_key, extent, jnp.float32)
    if shards:
        drawn = drawn * levels(stream_key, extent, shards, -0.22, 0.18)
    return jnp.clip(drawn, -most, most).astype(held_as)


def setup_inputs(seed: int = 0) -> dict:
    keys = jax.random.split(jax.random.key(seed), 5)
    tokens = scatter_about(keys[0], (TOKENS, D), 1.0, 6.0, ((0, 128),))
    routes_keys = jax.random.split(jax.random.fold_in(keys[1], 1), TOKENS // TOK_DEV)
    routes_turns = jax.random.permutation(jax.random.fold_in(keys[1], 3), TOKENS // TOK_DEV)
    routes = jax.vmap(lambda own, number: assign_block(jax.random.fold_in(keys[1], 2), own, number, TOK_DEV, EXPERTS, TOP, CAP, 1))(routes_keys, routes_turns).reshape((TOKENS, TOP))
    route_weights = jnp.clip(0.1 + 0.9 * jax.random.uniform(keys[2], (TOKENS, TOP), jnp.float32) ** levels(keys[2], (TOKENS, TOP), ((0, 128),), -0.2, 0.2), 0.1, 1.0)
    learner_weights = draw_learner_weights(jax.random.fold_in(keys[4], 71), 0)
    return {"tokens": tokens, "routes": routes, "route_weights": route_weights, "learner_weights": learner_weights}


def reference(tokens, routes, route_weights, learner_weights):
    block_ids = routes.reshape(N_EXPERT, TOK_DEV * TOP)
    one_hot = (block_ids[:, :, None] == jnp.arange(EXPERTS, dtype=jnp.int32)[None, None, :]).astype(jnp.int32)
    slot_rank = (jnp.sum(jnp.cumsum(one_hot, axis=1) * one_hot, axis=2) - 1).astype(jnp.int32)
    source_of = jnp.broadcast_to(jnp.arange(N_EXPERT, dtype=jnp.int32)[:, None], block_ids.shape)
    token_of = source_of * TOK_DEV + jnp.arange(TOK_DEV * TOP, dtype=jnp.int32)[None, :] // TOP
    slot_list = jnp.full((EXPERTS, N_EXPERT, CAP), TOKENS, jnp.int32).at[block_ids, source_of, slot_rank].set(token_of)
    padded = jnp.concatenate([tokens, jnp.zeros((1, D), tokens.dtype)], axis=0)

    def per_expert(inputs):
        weight, listed = inputs
        gathered_rows = padded[listed.reshape(-1)]
        return jnp.dot(gathered_rows, weight, preferred_element_type=jnp.float32).astype(jnp.bfloat16)

    outputs = lax.map(per_expert, (learner_weights, slot_list))
    picked = outputs.reshape(EXPERTS, N_EXPERT, CAP, FF)[block_ids, source_of, slot_rank]
    weights = route_weights.reshape(N_EXPERT, TOK_DEV * TOP, 1)
    combined = jnp.sum((picked.astype(jnp.float32) * weights).reshape(TOKENS, TOP, FF), axis=1).astype(jnp.bfloat16)
    expert_amax = jnp.max(jnp.abs(learner_weights), axis=(1, 2)).astype(jnp.float32)
    return combined, expert_amax
```

```python
import jax
import jax.numpy as jnp
from jax import lax
from jax.experimental import pallas as pl
from jax.experimental.pallas import tpu as pltpu
from jax.sharding import PartitionSpec as P

MESH = pl.DeviceIdType.MESH
BF = jnp.bfloat16
F32 = jnp.float32
NX, NZ, NY = 4, 8, 4
EXPERTS, DEPTH, WIDTH, TOP = 128, 32, 384, 8
HALF = 16
LANES = 128
COLS = NY * NZ * HALF


def offset_of(j):
    return jnp.where(j == 0, 2, jnp.where(j == 1, 1, jnp.where(j == 2, 3, 0)))


def kernel(
    tok_ref, route_ref, rw_ref, w_hbm, out_ref, amax_ref,
    w_ref, wt, st, dt, tb, rz, ry, tx, xf, mt, mz, ms, my, mf,
    am_rows, am_send, am_z, am_y, am_x, am_c,
    pf, pa, xa, rl, sl, rs, ss, qb, xb, sz, ao, za, ysa, ysb, ya, yb,
    w_sem, s_tz, r_tz, s_mz, r_mz, s_ty, r_ty, s_my, r_my, s_tx, r_tx, s_mx, r_mx, s_tc, r_tc,
    s_az, r_az, s_ay, r_ay, s_ax, r_ax, s_ac, r_ac,
    s_xa, r_xa, s_rl, r_rl, s_rs, r_rs, s_xb, r_xb, s_za, r_za, s_ya, r_ya, s_yb, r_yb,
):
    e = lax.axis_index("expert")
    t = lax.axis_index("tensor")
    x = lax.rem(e, NX)
    z = lax.rem(e // NX, NZ)
    y = e // (NX * NZ)
    core = lax.rem(t, 2)
    low = t // 2

    def at(yy, zz, xx):
        return (yy * NZ + zz) * NX + xx

    def zp(o):
        return (at(y, lax.rem(z + o, NZ), x), t)

    def yp(o):
        return (at(lax.rem(y + o, NY), z, x), t)

    def xp(o):
        return (at(y, z, lax.rem(x + o, NX)), t)

    sibling = (e, low * 2 + (1 - core))
    across = (e, (1 - low) * 2 + core)

    def remote(src, dst, ssem, rsem, device):
        return pltpu.make_async_remote_copy(
            src_ref=src, dst_ref=dst, send_sem=ssem, recv_sem=rsem, device_id=device, device_id_type=MESH
        )

    load_w = pltpu.make_async_copy(w_hbm, w_ref, w_sem)
    load_w.start()

    barrier = pltpu.get_barrier_semaphore()
    peers = [zp(o) for o in range(1, NZ)] + [yp(o) for o in range(1, NY)] + [xp(o) for o in range(1, NX)]
    peers += [sibling, across]
    for device in peers:
        pl.semaphore_signal(barrier, inc=1, device_id=device, device_id_type=MESH)

    rows = pl.ds(pl.multiple_of(core * HALF, HALF), HALF)
    for zz in range(NZ):
        for yy in range(NY):
            tb[zz, yy] = tok_ref[rows, (yy * NZ + zz) * LANES:(yy * NZ + zz + 1) * LANES]
    place = (
        lax.broadcasted_iota(jnp.int32, (HALF, LANES), 1)
        == lax.broadcasted_iota(jnp.int32, (HALF, LANES), 0) + z * HALF
    ).astype(F32)
    turn = (((0,), (0,)), ((), ()))
    mt[0:TOP] = lax.dot_general(
        route_ref[rows, :].astype(F32), place, turn, precision=lax.Precision.HIGHEST, preferred_element_type=F32
    )
    mt[TOP:2 * TOP] = lax.dot_general(
        rw_ref[rows, :], place, turn, precision=lax.Precision.HIGHEST, preferred_element_type=F32
    )
    pl.semaphore_wait(barrier, len(peers))

    def tz(o):
        return remote(tb.at[lax.rem(z + o, NZ)], rz.at[z], s_tz.at[o - 1], r_tz.at[o - 1], zp(o))

    def tz_in(o):
        return remote(tb.at[z], rz.at[lax.rem(z + NZ - o, NZ)], s_tz.at[o - 1], r_tz.at[o - 1], zp(o))

    def mzc(o):
        return remote(mt, mz.at[o - 1], s_mz.at[o - 1], r_mz.at[o - 1], zp(o))

    for o in (4, 3, 5, 2, 6, 1, 7):
        mzc(o).start()
        tz(o).start()
    rz[z] = tb[z]

    load_w.wait()

    def turn_w(i, _):
        r = pl.multiple_of(i * 256, 256)
        block = w_ref[pl.ds(r, 256), :]
        wt[:, pl.ds(r, 256)] = block.T
        big = jnp.abs(block)
        big = jnp.maximum(jnp.maximum(big[:, 0:128], big[:, 128:256]), big[:, 256:384])
        am_rows[pl.ds(pl.multiple_of(i * 8, 8), 8), :] = jnp.max(big.astype(F32).reshape(8, DEPTH, LANES), axis=1)
        return 0

    lax.fori_loop(0, 16, turn_w, 0)
    am_send[0] = jnp.max(am_rows[...].T.reshape(16, 8, LANES), axis=0)

    for o in range(1, NZ):
        mzc(o).wait_recv()
    gathered = mt[...]
    for o in range(1, NZ):
        gathered = gathered + mz[o - 1]
    ms[...] = gathered
    my[y] = gathered
    for o in range(1, NZ):
        tz_in(o).wait_recv()

    def tyc(o):
        return remote(rz.at[:, lax.rem(y + o, NY)], ry.at[y], s_ty.at[o - 1], r_ty.at[o - 1], yp(o))

    def ty_in(o):
        return remote(rz.at[:, y], ry.at[lax.rem(y + NY - o, NY)], s_ty.at[o - 1], r_ty.at[o - 1], yp(o))

    def myc(o):
        return remote(ms, my.at[y], s_my.at[o - 1], r_my.at[o - 1], yp(o))

    def my_in(o):
        return remote(ms, my.at[lax.rem(y + NY - o, NY)], s_my.at[o - 1], r_my.at[o - 1], yp(o))

    for o in (2, 1, 3):
        myc(o).start()
        tyc(o).start()
    for zz in range(NZ):
        ry[y, zz] = rz[zz, y]
    for o in range(1, NY):
        my_in(o).wait_recv()
        ty_in(o).wait_recv()

    def mxc(o):
        return remote(my, mf.at[core, x], s_mx.at[o - 1], r_mx.at[o - 1], xp(o))

    def mx_in(o):
        return remote(my, mf.at[core, lax.rem(x + NX - o, NX)], s_mx.at[o - 1], r_mx.at[o - 1], xp(o))

    def txc(o):
        return remote(tx.at[lax.rem(x + o, NX)], xf.at[core, x], s_tx.at[o - 1], r_tx.at[o - 1], xp(o))

    def tx_in(o):
        return remote(tx.at[x], xf.at[core, lax.rem(x + NX - o, NX)], s_tx.at[o - 1], r_tx.at[o - 1], xp(o))

    for o in (2, 1, 3):
        mxc(o).start()
    mf[core, x] = my[...]
    for yy in range(NY):
        turned = ry[yy].reshape(NZ * HALF, LANES).T
        for xx in range(NX):
            tx[xx, :, yy * 128:(yy + 1) * 128] = turned[xx * DEPTH:(xx + 1) * DEPTH, :]
    for o in (2, 1, 3):
        txc(o).start()
    xf[core, x] = tx[x]
    for o in range(1, NX):
        mx_in(o).wait_recv()
        tx_in(o).wait_recv()

    def mcc(h):
        return remote(mf.at[h], mf.at[h], s_tc.at[0], r_tc.at[0], sibling)

    def tcc(h):
        return remote(xf.at[h], xf.at[h], s_tc.at[1], r_tc.at[1], sibling)

    mcc(core).start()
    tcc(core).start()

    def compute(i):
        b = lax.rem(i, 2)
        h = lax.rem(core + b, 2)
        xx = lax.rem(x + offset_of(i // 2), NX)
        ids = lax.broadcasted_iota(jnp.int32, (EXPERTS, LANES), 0).astype(F32)
        for yy in range(NY):
            dense = jnp.zeros((EXPERTS, LANES), F32)
            meta = mf[h, xx, yy]
            for k in range(TOP):
                dense = jnp.where(ids == meta[k:k + 1, :], meta[TOP + k:TOP + k + 1, :], dense)
            dt[:, yy * LANES:(yy + 1) * LANES] = dense
        features = xf[h, xx].astype(F32)

        def spread(g, _):
            for j in range(8):
                row = dt[pl.ds(g * 8 + j, 1), :]
                st[pl.ds(pl.multiple_of(g * 256 + j * DEPTH, DEPTH), DEPTH), :] = (features * row).astype(BF)
            return 0

        lax.fori_loop(0, 16, spread, 0)
        part = jnp.dot(wt[...], st[...], preferred_element_type=F32).T
        for yy in range(NY):
            for zz in range(NZ):
                r = (yy * NZ + zz) * HALF
                pf[i, zz, yy] = part[r:r + HALF, :]

    def xac(j):
        return remote(pa.at[j], xa.at[j], s_xa.at[j], r_xa.at[j], xp(offset_of(j)))

    def ring_long(j, s):
        way = 1 - 2 * lax.rem(j, 2)
        return remote(sl.at[j, s - 1], rl.at[j, s - 1], s_rl.at[j, s - 1], r_rl.at[j, s - 1], zp(way + NZ))

    def ring_short(j, s):
        way = 1 - 2 * lax.rem(j, 2)
        return remote(ss.at[j, s - 1], rs.at[j, s - 1], s_rs.at[j, s - 1], r_rs.at[j, s - 1], zp(NZ - way))

    def ring_step(j, s):
        way = 1 - 2 * lax.rem(j, 2)
        held = pf[2 * j + 1, lax.rem(z + way * (5 - s) + NZ, NZ)]
        if s > 1:
            ring_long(j, s - 1).wait_recv()
            held = held + rl[j, s - 2].astype(F32)
        sl[j, s - 1] = held.astype(BF)
        ring_long(j, s).start()
        if s < 4:
            held = pf[2 * j + 1, lax.rem(z - way * (4 - s) + NZ, NZ)]
            if s > 1:
                ring_short(j, s - 1).wait_recv()
                held = held + rs[j, s - 2].astype(F32)
            ss[j, s - 1] = held.astype(BF)
            ring_short(j, s).start()

    def xbc(j):
        return remote(qb.at[j], xb.at[j], s_xb.at[j], r_xb.at[j], xp(offset_of(j)))

    def ring_end(j):
        ring_long(j, 4).wait_recv()
        ring_short(j, 3).wait_recv()
        qb[j] = pf[2 * j + 1, z] + rl[j, 3].astype(F32) + rs[j, 2].astype(F32)

        @pl.when(j < 3)
        def _():
            xbc(j).start()

    def zac(o):
        return remote(sz.at[lax.rem(z + o, NZ)], za.at[o - 1], s_za.at[o - 1], r_za.at[o - 1], zp(o))

    def azc(o):
        return remote(am_send.at[0], am_z.at[o - 1], s_az.at[o - 1], r_az.at[o - 1], zp(o))

    def ayc(o):
        return remote(am_send.at[1], am_y.at[o - 1], s_ay.at[o - 1], r_ay.at[o - 1], yp(o))

    def axc(o):
        return remote(am_send.at[2], am_x.at[o - 1], s_ax.at[o - 1], r_ax.at[o - 1], xp(o))

    def acc(k):
        return remote(am_send.at[3 + k], am_c.at[k], s_ac.at[k], r_ac.at[k], sibling if k == 0 else across)

    def slot(i, _):
        @pl.when(i == 1)
        def _():
            mcc(1 - core).wait_recv()
            tcc(1 - core).wait_recv()

        @pl.when(i < 8)
        def _():
            compute(i)

        b = lax.rem(i, 2)

        @pl.when((b == 0) & (i < 6))
        def _():
            j = i // 2
            pa[j] = pf[i].astype(BF)
            xac(j).start()

        @pl.when((b == 1) & (i <= 7))
        def _():
            ring_step((i - 1) // 2, 1)

        @pl.when((b == 0) & (i >= 2) & (i <= 8))
        def _():
            ring_step((i - 2) // 2, 2)

        @pl.when((b == 1) & (i >= 3) & (i <= 9))
        def _():
            ring_step((i - 3) // 2, 3)

        @pl.when((b == 0) & (i >= 4) & (i <= 10))
        def _():
            ring_step((i - 4) // 2, 4)

        @pl.when((b == 1) & (i >= 5) & (i <= 11))
        def _():
            ring_end((i - 5) // 2)

        @pl.when(i == 7)
        def _():
            for j in range(3):
                xac(j).wait_recv()
            for zz in range(NZ):
                total = pf[6, zz] + xa[0, zz].astype(F32) + xa[1, zz].astype(F32) + xa[2, zz].astype(F32)
                pf[6, zz] = total
                sz[zz] = total.astype(BF)
            for o in (4, 3, 5, 2, 6, 1, 7):
                zac(o).start()

        @pl.when(i == 0)
        def _():
            for o in range(1, NZ):
                azc(o).start()

        @pl.when(i == 2)
        def _():
            top = am_send[0]
            for o in range(1, NZ):
                azc(o).wait_recv()
                top = jnp.maximum(top, am_z[o - 1])
            am_send[1] = top
            for o in range(1, NY):
                ayc(o).start()

        @pl.when(i == 4)
        def _():
            top = am_send[1]
            for o in range(1, NY):
                ayc(o).wait_recv()
                top = jnp.maximum(top, am_y[o - 1])
            am_send[2] = top
            for o in range(1, NX):
                axc(o).start()

        @pl.when(i == 6)
        def _():
            top = am_send[2]
            for o in range(1, NX):
                axc(o).wait_recv()
                top = jnp.maximum(top, am_x[o - 1])
            am_send[3] = top
            acc(0).start()

        @pl.when(i == 8)
        def _():
            acc(0).wait_recv()
            am_send[4] = jnp.maximum(am_send[3], am_c[0])
            acc(1).start()

        return 0

    lax.fori_loop(0, 12, slot, 0)

    def yac(o):
        return remote(ysa.at[lax.rem(y + o, NY)], ya.at[o - 1], s_ya.at[o - 1], r_ya.at[o - 1], yp(o))

    def ybc(o):
        return remote(ysb.at[lax.rem(y + o, NY)], yb.at[o - 1], s_yb.at[o - 1], r_yb.at[o - 1], yp(o))

    total = pf[6, z]
    for o in range(1, NZ):
        zac(o).wait_recv()
        total = total + za[o - 1].astype(F32)
    ysa[...] = total
    for o in (2, 1, 3):
        yac(o).start()
    total = qb[3]
    for j in range(3):
        xbc(j).wait_recv()
        total = total + xb[j]
    ysb[...] = total
    for o in (2, 1, 3):
        ybc(o).start()

    acc(1).wait_recv()
    top = jnp.max(jnp.maximum(am_send[4], am_c[1]), axis=0, keepdims=True)
    mine = lax.broadcasted_iota(jnp.int32, (1, LANES), 1) == e
    amax_ref[0] = jnp.max(jnp.where(mine, top, 0.0))

    total = ysa[y]
    for o in range(1, NY):
        yac(o).wait_recv()
        total = total + ya[o - 1]
    out_ref[rows, :] = total.astype(BF)
    total = ysb[y]
    for o in range(1, NY):
        ybc(o).wait_recv()
        total = total + yb[o - 1]
    out_ref[pl.ds(pl.multiple_of((1 - core) * HALF, HALF), HALF), :] = total.astype(BF)

    for o in range(1, NZ):
        tz(o).wait_send()
        mzc(o).wait_send()
        azc(o).wait_send()
        zac(o).wait_send()
    for o in range(1, NY):
        tyc(o).wait_send()
        myc(o).wait_send()
        ayc(o).wait_send()
        yac(o).wait_send()
        ybc(o).wait_send()
    for o in range(1, NX):
        txc(o).wait_send()
        mxc(o).wait_send()
        axc(o).wait_send()
    mcc(core).wait_send()
    tcc(core).wait_send()
    for k in range(2):
        acc(k).wait_send()
    for j in range(3):
        xac(j).wait_send()
        xbc(j).wait_send()
    for j in range(4):
        for s in range(1, 5):
            ring_long(j, s).wait_send()
            if s < 4:
                ring_short(j, s).wait_send()


def shards(tokens, routes, route_weights, learner_weights):
    vmem = pl.BlockSpec(memory_space=pltpu.VMEM)
    block = (NY, HALF, WIDTH)

    def dma(*shape):
        return [pltpu.SemaphoreType.DMA(shape), pltpu.SemaphoreType.DMA(shape)]

    combined, amax = pl.pallas_call(
        kernel,
        out_shape=(
            jax.ShapeDtypeStruct((2 * HALF, WIDTH), BF),
            jax.ShapeDtypeStruct((1,), F32),
        ),
        in_specs=[vmem, vmem, vmem, pl.BlockSpec(memory_space=pl.ANY)],
        out_specs=(vmem, pl.BlockSpec(memory_space=pltpu.SMEM)),
        scratch_shapes=[
            pltpu.VMEM((EXPERTS * DEPTH, WIDTH), BF),
            pltpu.VMEM((WIDTH, EXPERTS * DEPTH), BF),
            pltpu.VMEM((EXPERTS * DEPTH, COLS), BF),
            pltpu.VMEM((EXPERTS, COLS), F32),
            pltpu.VMEM((NZ, NY, HALF, LANES), BF),
            pltpu.VMEM((NZ, NY, HALF, LANES), BF),
            pltpu.VMEM((NY, NZ, HALF, LANES), BF),
            pltpu.VMEM((NX, DEPTH, COLS), BF),
            pltpu.VMEM((2, NX, DEPTH, COLS), BF),
            pltpu.VMEM((2 * TOP, LANES), F32),
            pltpu.VMEM((NZ - 1, 2 * TOP, LANES), F32),
            pltpu.VMEM((2 * TOP, LANES), F32),
            pltpu.VMEM((NY, 2 * TOP, LANES), F32),
            pltpu.VMEM((2, NX, NY, 2 * TOP, LANES), F32),
            pltpu.VMEM((EXPERTS, LANES), F32),
            pltpu.VMEM((5, 8, LANES), F32),
            pltpu.VMEM((NZ - 1, 8, LANES), F32),
            pltpu.VMEM((NY - 1, 8, LANES), F32),
            pltpu.VMEM((NX - 1, 8, LANES), F32),
            pltpu.VMEM((2, 8, LANES), F32),
            pltpu.VMEM((8, NZ, *block), F32),
            pltpu.VMEM((3, NZ, *block), BF),
            pltpu.VMEM((3, NZ, *block), BF),
            pltpu.VMEM((4, 4, *block), BF),
            pltpu.VMEM((4, 4, *block), BF),
            pltpu.VMEM((4, 3, *block), BF),
            pltpu.VMEM((4, 3, *block), BF),
            pltpu.VMEM((4, *block), F32),
            pltpu.VMEM((3, *block), F32),
            pltpu.VMEM((NZ, *block), BF),
            pltpu.VMEM(block, F32),
            pltpu.VMEM((NZ - 1, *block), BF),
            pltpu.VMEM(block, F32),
            pltpu.VMEM(block, F32),
            pltpu.VMEM((NY - 1, HALF, WIDTH), F32),
            pltpu.VMEM((NY - 1, HALF, WIDTH), F32),
            pltpu.SemaphoreType.DMA,
            *dma(NZ - 1), *dma(NZ - 1), *dma(NY - 1), *dma(NY - 1), *dma(NX - 1), *dma(NX - 1), *dma(2),
            *dma(NZ - 1), *dma(NY - 1), *dma(NX - 1), *dma(2),
            *dma(3), *dma(4, 4), *dma(4, 3), *dma(3), *dma(NZ - 1), *dma(NY - 1), *dma(NY - 1),
        ],
        compiler_params=pltpu.CompilerParams(
            collective_id=0, has_side_effects=True, vmem_limit_bytes=60 * 2**20
        ),
        name="relay",
    )(tokens, routes, route_weights, learner_weights.reshape(EXPERTS * DEPTH, WIDTH))
    return combined, amax


def solution(mesh):
    return jax.shard_map(
        shards,
        mesh=mesh,
        in_specs=(
            P("expert", None),
            P("expert", None),
            P("expert", None),
            P(None, "expert", "tensor"),
        ),
        out_specs=(P("expert", "tensor"), P("expert")),
        check_vma=False,
    )
```

```python
import jax
import jax.numpy as jnp
from jax import lax
from jax.experimental import pallas as pl
from jax.experimental.pallas import tpu as pltpu
from jax.sharding import PartitionSpec as P

MESH = pl.DeviceIdType.MESH
BF = jnp.bfloat16
F32 = jnp.float32
NX, NZ, NY = 4, 8, 4
EXPERTS, DEPTH, WIDTH, TOP = 128, 32, 384, 8
HALF = 16
LANES = 128
COLS = NY * NZ * HALF


A_HALF = 0
ORDER = ((0, 0), (0, 2), (0, 1), (0, 3), (1, 2), (1, 1), (1, 3), (1, 0))
B_RINGS = ((4, 6, 7, 8, 9), (5, 7, 8, 9, 10), (6, 7, 8, 9, 10), (7, 8, 9, 10, 11))
A_RING = (7, 8, 9, 10, 11)
SECOND = 3
AMAX = (0, 4, 6, 8, 9)
STEPS = 12
FAR_FIRST = (4, 5, 3, 6, 2, 7, 1, 0)
SENT = {2: 0, 1: 1, 3: 2}


def pick(i, values):
    found = jnp.int32(values[0])
    for n, value in enumerate(values[1:]):
        found = jnp.where(i == n + 1, value, found)
    return found


def kernel(
    tok_ref, route_ref, rw_ref, w_hbm, out_ref, amax_ref,
    w_ref, wt, st, dt, tb, rz, ry, tx, xf, mt, mz, ms, my, mf,
    am_rows, am_send, am_z, am_y, am_x, am_c,
    pf, pa, xa, rl, sl, rs, ss, qb, xb, ysa, ysb, ya, yb,
    w_sem, s_tz, r_tz, s_mz, r_mz, s_ty, r_ty, s_my, r_my, s_tx, r_tx, s_mx, r_mx, s_tc, r_tc, s_mc, r_mc,
    s_az, r_az, s_ay, r_ay, s_ax, r_ax, s_ac, r_ac,
    s_xa, r_xa, s_rl, r_rl, s_rs, r_rs, s_xb, r_xb, s_ya, r_ya, s_yb, r_yb,
):
    e = lax.axis_index("expert")
    t = lax.axis_index("tensor")
    x = lax.rem(e, NX)
    z = lax.rem(e // NX, NZ)
    y = e // (NX * NZ)
    core = lax.rem(t, 2)
    low = t // 2

    def at(yy, zz, xx):
        return (yy * NZ + zz) * NX + xx

    def zp(o):
        return (at(y, lax.rem(z + o, NZ), x), t)

    def yp(o):
        return (at(lax.rem(y + o, NY), z, x), t)

    def xp(o):
        return (at(y, z, lax.rem(x + o, NX)), t)

    sibling = (e, low * 2 + (1 - core))
    across = (e, (1 - low) * 2 + core)

    def remote(src, dst, ssem, rsem, device):
        return pltpu.make_async_remote_copy(
            src_ref=src, dst_ref=dst, send_sem=ssem, recv_sem=rsem, device_id=device, device_id_type=MESH
        )

    load_w = pltpu.make_async_copy(w_hbm, w_ref, w_sem)
    load_w.start()

    barrier = pltpu.get_barrier_semaphore()
    peers = [zp(o) for o in range(1, NZ)] + [yp(o) for o in range(1, NY)] + [xp(o) for o in range(1, NX)]
    peers += [sibling, across]
    for device in peers:
        pl.semaphore_signal(barrier, inc=1, device_id=device, device_id_type=MESH)

    rows = pl.ds(pl.multiple_of(core * HALF, HALF), HALF)
    for zz in range(NZ):
        for yy in range(NY):
            tb[zz, yy] = tok_ref[rows, (yy * NZ + zz) * LANES:(yy * NZ + zz + 1) * LANES]
    place = (
        lax.broadcasted_iota(jnp.int32, (2 * HALF, LANES), 1)
        == lax.broadcasted_iota(jnp.int32, (2 * HALF, LANES), 0) + (z - core) * HALF
    ) & (lax.broadcasted_iota(jnp.int32, (2 * HALF, LANES), 1) // HALF == z)
    place = place.astype(F32)
    mt[0:TOP] = jnp.dot(route_ref[...].astype(F32), place, precision=lax.Precision.HIGHEST, preferred_element_type=F32)
    mt[TOP:2 * TOP] = jnp.dot(rw_ref[...], place, precision=lax.Precision.HIGHEST, preferred_element_type=F32)
    pl.semaphore_wait(barrier, len(peers))

    def tz(o):
        return remote(tb.at[lax.rem(z + o, NZ)], rz.at[z], s_tz.at[o - 1], r_tz.at[o - 1], zp(o))

    def tz_in(o):
        return remote(tb.at[z], rz.at[lax.rem(z + NZ - o, NZ)], s_tz.at[o - 1], r_tz.at[o - 1], zp(o))

    def mzc(o):
        return remote(mt, mz.at[o - 1], s_mz.at[o - 1], r_mz.at[o - 1], zp(o))

    def tyc(oy, o):
        zs = lax.rem(z + NZ - o, NZ)
        src = (rz if o else tb).at[zs, lax.rem(y + oy, NY)]
        return remote(src, ry.at[y, zs], s_ty.at[oy - 1, o], r_ty.at[oy - 1, o], yp(oy))

    def ty_in(oy, o):
        zs = lax.rem(z + NZ - o, NZ)
        return remote(tb.at[z, y], ry.at[lax.rem(y + NY - oy, NY), zs], s_ty.at[oy - 1, o], r_ty.at[oy - 1, o], yp(oy))

    def myc(o):
        return remote(ms, my.at[y], s_my.at[o - 1], r_my.at[o - 1], yp(o))

    def my_in(o):
        return remote(ms, my.at[lax.rem(y + NY - o, NY)], s_my.at[o - 1], r_my.at[o - 1], yp(o))

    def mxc(ox, oy):
        ys = lax.rem(y + NY - oy, NY)
        return remote(my.at[ys], mf.at[core, x, ys], s_mx.at[ox - 1, oy], r_mx.at[ox - 1, oy], xp(ox))

    def mx_in(ox, oy):
        ys = lax.rem(y + NY - oy, NY)
        dst = mf.at[core, lax.rem(x + NX - ox, NX), ys]
        return remote(my.at[ys], dst, s_mx.at[ox - 1, oy], r_mx.at[ox - 1, oy], xp(ox))

    def txc(ox, oy):
        ys = lax.rem(y + NY - oy, NY)
        src = tx.at[lax.rem(x + ox, NX), ys]
        return remote(src, xf.at[core, x, ys], s_tx.at[ox - 1, oy], r_tx.at[ox - 1, oy], xp(ox))

    def tx_in(ox, oy):
        ys = lax.rem(y + NY - oy, NY)
        dst = xf.at[core, lax.rem(x + NX - ox, NX), ys]
        return remote(tx.at[x, ys], dst, s_tx.at[ox - 1, oy], r_tx.at[ox - 1, oy], xp(ox))

    def mcc(ox, h):
        part = mf.at[h, lax.rem(x + NX - ox, NX)]
        return remote(part, part, s_mc.at[ox], r_mc.at[ox], sibling)

    def tcc(ox, h):
        part = xf.at[h, lax.rem(x + NX - ox, NX)]
        return remote(part, part, s_tc.at[ox], r_tc.at[ox], sibling)

    for o in (4, 3, 5, 2, 6, 1, 7):
        mzc(o).start()
        tz(o).start()
    for oy in (2, 1, 3):
        tyc(oy, 0).start()
    ry[y, z] = tb[z, y]

    load_w.wait()

    def turn_w(i, _):
        r = pl.multiple_of(i * 256, 256)
        block = w_ref[pl.ds(r, 256), :]
        wt[:, pl.ds(r, 256)] = block.T
        big = jnp.abs(block)
        big = jnp.maximum(jnp.maximum(big[:, 0:128], big[:, 128:256]), big[:, 256:384])
        am_rows[pl.ds(pl.multiple_of(i * 8, 8), 8), :] = jnp.max(big.astype(F32).reshape(8, DEPTH, LANES), axis=1)
        return 0

    lax.fori_loop(0, 16, turn_w, 0)
    am_send[0] = jnp.max(am_rows[...].T.reshape(16, 8, LANES), axis=0)

    gathered = mt[...]
    for o in (1, 7, 2, 6, 3, 5, 4):
        tz_in(o).wait_recv()
        for oy in (2, 1, 3):
            tyc(oy, o).start()
        zs = lax.rem(z + NZ - o, NZ)
        ry[y, zs] = rz[zs, y]
        mzc(o).wait_recv()
        gathered = gathered + mz[o - 1]
    ms[...] = gathered
    my[y] = gathered
    for o in (2, 1, 3):
        myc(o).start()

    for oy in (0, 1, 3, 2):
        ys = lax.rem(y + NY - oy, NY)
        if oy:
            my_in(oy).wait_recv()
            for o in range(NZ):
                ty_in(oy, o).wait_recv()
        for ox in (2, 1, 3):
            mxc(ox, oy).start()
        mf[core, x, ys] = my[ys]
        turned = ry[ys].reshape(NZ * HALF, LANES).T
        for xx in range(NX):
            tx[xx, ys] = turned[xx * DEPTH:(xx + 1) * DEPTH, :]
        for ox in (2, 1, 3):
            txc(ox, oy).start()
        xf[core, x, ys] = tx[x, ys]
    mcc(0, core).start()
    tcc(0, core).start()

    def x_arrived():
        for ox in (1, 3, 2):
            for oy in range(NY):
                mx_in(ox, oy).wait_recv()
                tx_in(ox, oy).wait_recv()
            mcc(ox, core).start()
            tcc(ox, core).start()

    def core_arrived():
        for ox in range(NX):
            mcc(ox, 1 - core).wait_recv()
            tcc(ox, 1 - core).wait_recv()

    def compute(i):
        h = lax.rem(core + pick(i, [half for half, _ in ORDER]), 2)
        xx = lax.rem(x + pick(i, [off for _, off in ORDER]), NX)
        ids = lax.broadcasted_iota(jnp.int32, (EXPERTS, LANES), 0).astype(F32)
        for yy in range(NY):
            dense = jnp.zeros((EXPERTS, LANES), F32)
            meta = mf[h, xx, yy]
            for k in range(TOP):
                dense = jnp.where(ids == meta[k:k + 1, :], meta[TOP + k:TOP + k + 1, :], dense)
            dt[:, yy * LANES:(yy + 1) * LANES] = dense
        features = jnp.concatenate([xf[h, xx, yy] for yy in range(NY)], axis=1).astype(F32)

        for n in range(EXPERTS):
            st[n * DEPTH:(n + 1) * DEPTH, :] = (features * dt[n:n + 1, :]).astype(BF)
        part = jnp.dot(wt[...], st[...], preferred_element_type=F32).T
        for yy in range(NY):
            for zz in range(NZ):
                r = (yy * NZ + zz) * HALF
                pf[i, zz, yy] = part[r:r + HALF, :]

    a_steps = [i for i, (half, _) in enumerate(ORDER) if half == A_HALF]
    b_steps = [i for i, (half, _) in enumerate(ORDER) if half != A_HALF]
    a_own = next(i for i in a_steps if ORDER[i][1] == 0)
    b_own = next(n for n, i in enumerate(b_steps) if ORDER[i][1] == 0)
    ways = (1, -1, 1, -1, 1)

    def xac(off, p):
        k = SENT[off]
        part = pl.ds(4 * p, 4)
        return remote(pa.at[k, part], xa.at[k, part], s_xa.at[k, p], r_xa.at[k, p], xp(off))

    def held_block(j, rel):
        zz = lax.rem(z + rel, NZ)
        if j < 4:
            return pf[b_steps[j], zz]
        r = FAR_FIRST.index(rel)
        return pf[a_own, zz] + xa[0, r].astype(F32) + xa[1, r].astype(F32) + xa[2, r].astype(F32)

    def ring_long(j, s):
        return remote(sl.at[j, s - 1], rl.at[j, s - 1], s_rl.at[j, s - 1], r_rl.at[j, s - 1], zp(NZ + ways[j]))

    def ring_short(j, s):
        return remote(ss.at[j, s - 1], rs.at[j, s - 1], s_rs.at[j, s - 1], r_rs.at[j, s - 1], zp(NZ - ways[j]))

    def xbc(off):
        k = SENT[off]
        j = next(n for n, i in enumerate(b_steps) if ORDER[i][1] == off)
        return remote(qb.at[j], xb.at[k], s_xb.at[k], r_xb.at[k], xp(off))

    def ring_step(j, s):
        if j == 4 and s in (1, 3):
            for off in (1, 3, 2):
                xac(off, s // 2).wait_recv()
        block = held_block(j, (ways[j] * (5 - s)) % NZ)
        if s > 1:
            ring_long(j, s - 1).wait_recv()
            block = block + rl[j, s - 2].astype(F32)
        sl[j, s - 1] = block.astype(BF)
        ring_long(j, s).start()
        if s < 4:
            block = held_block(j, (-ways[j] * (4 - s)) % NZ)
            if s > 1:
                ring_short(j, s - 1).wait_recv()
                block = block + rs[j, s - 2].astype(F32)
            ss[j, s - 1] = block.astype(BF)
            ring_short(j, s).start()

    def ring_end(j):
        ring_long(j, 4).wait_recv()
        ring_short(j, 3).wait_recv()
        qb[j] = held_block(j, 0) + rl[j, 3].astype(F32) + rs[j, 2].astype(F32)
        if j < 4 and ORDER[b_steps[j]][1]:
            xbc(ORDER[b_steps[j]][1]).start()

    def azc(o):
        return remote(am_send.at[0], am_z.at[o - 1], s_az.at[o - 1], r_az.at[o - 1], zp(o))

    def ayc(o):
        return remote(am_send.at[1], am_y.at[o - 1], s_ay.at[o - 1], r_ay.at[o - 1], yp(o))

    def axc(o):
        return remote(am_send.at[2], am_x.at[o - 1], s_ax.at[o - 1], r_ax.at[o - 1], xp(o))

    def acc(k):
        return remote(am_send.at[3 + k], am_c.at[k], s_ac.at[k], r_ac.at[k], sibling if k == 0 else across)

    def amax_stage(n):
        top = am_send[n - 1] if n else None
        for o in range(1, NZ) if n == 1 else range(1, NY) if n == 2 else range(1, NX) if n == 3 else ():
            (azc, ayc, axc)[n - 1](o).wait_recv()
            top = jnp.maximum(top, (am_z, am_y, am_x)[n - 1][o - 1])
        if n == 4:
            acc(0).wait_recv()
            top = jnp.maximum(top, am_c[0])
        if n:
            am_send[n] = top
        if n < 3:
            for o in range(1, (NZ, NY, NX)[n]):
                (azc, ayc, axc)[n](o).start()
        else:
            acc(n - 3).start()

    def after(i):
        if i < 8 and i in a_steps and ORDER[i][1]:
            k = SENT[ORDER[i][1]]
            for r, rel in enumerate(FAR_FIRST):
                pa[k, r] = pf[i, lax.rem(z + rel, NZ)].astype(BF)
                if r == 3:
                    xac(ORDER[i][1], 0).start()
        if i == SECOND:
            for n in a_steps:
                if ORDER[n][1]:
                    xac(ORDER[n][1], 1).start()
        for s in (1, 0, 5, 4, 3, 2):
            if s == 0 and i == 0:
                x_arrived()
            for j, when in enumerate((*B_RINGS, A_RING)):
                if s and when[s - 1] == i:
                    ring_end(j) if s == 5 else ring_step(j, s)
        if i in AMAX:
            amax_stage(AMAX.index(i))

    def step(i, _):
        @pl.when(i == 2)
        def _():
            core_arrived()

        @pl.when(i < 8)
        def _():
            compute(i)

        for n in range(STEPS):
            pl.when(i == n)(lambda n=n: after(n))
        return 0

    lax.fori_loop(0, STEPS, step, 0)

    def yac(o):
        return remote(ysa.at[lax.rem(y + o, NY)], ya.at[o - 1], s_ya.at[o - 1], r_ya.at[o - 1], yp(o))

    def ybc(o):
        return remote(ysb.at[lax.rem(y + o, NY)], yb.at[o - 1], s_yb.at[o - 1], r_yb.at[o - 1], yp(o))

    total = qb[b_own]
    for off in (1, 3, 2):
        xbc(off).wait_recv()
        total = total + xb[SENT[off]]
    ysb[...] = total
    for o in (2, 1, 3):
        ybc(o).start()
    ysa[...] = qb[4]
    for o in (2, 1, 3):
        yac(o).start()

    acc(1).wait_recv()
    top = jnp.max(jnp.maximum(am_send[4], am_c[1]), axis=0, keepdims=True)
    mine = lax.broadcasted_iota(jnp.int32, (1, LANES), 1) == e
    amax_ref[0] = jnp.max(jnp.where(mine, top, 0.0))

    for source, copies, arrived, other in ((ysb, ybc, yb, 1 - A_HALF), (ysa, yac, ya, A_HALF)):
        total = source[y]
        for o in range(1, NY):
            copies(o).wait_recv()
            total = total + arrived[o - 1]
        half = lax.rem(core + other, 2)
        out_ref[pl.ds(pl.multiple_of(half * HALF, HALF), HALF), :] = total.astype(BF)

    for o in range(1, NZ):
        tz(o).wait_send()
        mzc(o).wait_send()
        azc(o).wait_send()
    for oy in range(1, NY):
        for o in range(NZ):
            tyc(oy, o).wait_send()
        myc(oy).wait_send()
        ayc(oy).wait_send()
        yac(oy).wait_send()
        ybc(oy).wait_send()
    for ox in range(1, NX):
        for oy in range(NY):
            txc(ox, oy).wait_send()
            mxc(ox, oy).wait_send()
        axc(ox).wait_send()
        xac(ox, 0).wait_send()
        xac(ox, 1).wait_send()
        xbc(ox).wait_send()
    for ox in range(NX):
        mcc(ox, core).wait_send()
        tcc(ox, core).wait_send()
    for k in range(2):
        acc(k).wait_send()
    for j in range(5):
        for s in range(1, 5):
            ring_long(j, s).wait_send()
            if s < 4:
                ring_short(j, s).wait_send()


def shards(tokens, routes, route_weights, learner_weights):
    vmem = pl.BlockSpec(memory_space=pltpu.VMEM)
    block = (NY, HALF, WIDTH)

    def dma(*shape):
        return [pltpu.SemaphoreType.DMA(shape), pltpu.SemaphoreType.DMA(shape)]

    combined, amax = pl.pallas_call(
        kernel,
        out_shape=(
            jax.ShapeDtypeStruct((2 * HALF, WIDTH), BF),
            jax.ShapeDtypeStruct((1,), F32),
        ),
        in_specs=[vmem, vmem, vmem, pl.BlockSpec(memory_space=pl.ANY)],
        out_specs=(vmem, pl.BlockSpec(memory_space=pltpu.SMEM)),
        scratch_shapes=[
            pltpu.VMEM((EXPERTS * DEPTH, WIDTH), BF),
            pltpu.VMEM((WIDTH, EXPERTS * DEPTH), BF),
            pltpu.VMEM((EXPERTS * DEPTH, COLS), BF),
            pltpu.VMEM((EXPERTS, COLS), F32),
            pltpu.VMEM((NZ, NY, HALF, LANES), BF),
            pltpu.VMEM((NZ, NY, HALF, LANES), BF),
            pltpu.VMEM((NY, NZ, HALF, LANES), BF),
            pltpu.VMEM((NX, NY, DEPTH, LANES), BF),
            pltpu.VMEM((2, NX, NY, DEPTH, LANES), BF),
            pltpu.VMEM((2 * TOP, LANES), F32),
            pltpu.VMEM((NZ - 1, 2 * TOP, LANES), F32),
            pltpu.VMEM((2 * TOP, LANES), F32),
            pltpu.VMEM((NY, 2 * TOP, LANES), F32),
            pltpu.VMEM((2, NX, NY, 2 * TOP, LANES), F32),
            pltpu.VMEM((EXPERTS, LANES), F32),
            pltpu.VMEM((5, 8, LANES), F32),
            pltpu.VMEM((NZ - 1, 8, LANES), F32),
            pltpu.VMEM((NY - 1, 8, LANES), F32),
            pltpu.VMEM((NX - 1, 8, LANES), F32),
            pltpu.VMEM((2, 8, LANES), F32),
            pltpu.VMEM((8, NZ, *block), F32),
            pltpu.VMEM((3, NZ, *block), BF),
            pltpu.VMEM((3, NZ, *block), BF),
            pltpu.VMEM((5, 4, *block), BF),
            pltpu.VMEM((5, 4, *block), BF),
            pltpu.VMEM((5, 3, *block), BF),
            pltpu.VMEM((5, 3, *block), BF),
            pltpu.VMEM((5, *block), F32),
            pltpu.VMEM((3, *block), F32),
            pltpu.VMEM(block, F32),
            pltpu.VMEM(block, F32),
            pltpu.VMEM((NY - 1, HALF, WIDTH), F32),
            pltpu.VMEM((NY - 1, HALF, WIDTH), F32),
            pltpu.SemaphoreType.DMA,
            *dma(NZ - 1), *dma(NZ - 1), *dma(NY - 1, NZ), *dma(NY - 1), *dma(NX - 1, NY), *dma(NX - 1, NY), *dma(NX), *dma(NX),
            *dma(NZ - 1), *dma(NY - 1), *dma(NX - 1), *dma(2),
            *dma(3, 2), *dma(5, 4), *dma(5, 3), *dma(3), *dma(NY - 1), *dma(NY - 1),
        ],
        compiler_params=pltpu.CompilerParams(
            collective_id=0, has_side_effects=True, vmem_limit_bytes=60 * 2**20
        ),
        name="relay",
    )(tokens, routes.T, route_weights.T, learner_weights.reshape(EXPERTS * DEPTH, WIDTH))
    return combined, amax


def solution(mesh):
    return jax.shard_map(
        shards,
        mesh=mesh,
        in_specs=(
            P("expert", None),
            P("expert", None),
            P("expert", None),
            P(None, "expert", "tensor"),
        ),
        out_specs=(P("expert", "tensor"), P("expert")),
        check_vma=False,
    )
```

```python
import jax
import jax.numpy as jnp
from jax import lax
from jax.experimental import pallas as pl
from jax.experimental.pallas import tpu as pltpu
from jax.sharding import PartitionSpec as P

MESH = pl.DeviceIdType.MESH
BF = jnp.bfloat16
F32 = jnp.float32
NX, NZ, NY = 4, 8, 4
EXPERTS, DEPTH, WIDTH, TOP = 128, 32, 384, 8
HALF = 16
LANES = 128
COLS = NY * NZ * HALF


ORDER = ((0, 0), (0, 1), (0, 3), (0, 2), (1, 1), (1, 3), (1, 2), (1, 0))
RINGS = ((3, 5, 6, 7, 8), (6, 7, 8, 9, 10), (6, 7, 8, 9, 10), (7, 8, 9, 10, 11))
SECOND = (4, 6)
AMAX = (0, 4, 6, 8, 9)
STEPS = 12
FAR_FIRST = (4, 5, 3, 6, 2, 7, 1, 0)
SENT = {1: 0, 3: 1}


def pick(i, values):
    found = jnp.int32(values[0])
    for n, value in enumerate(values[1:]):
        found = jnp.where(i == n + 1, value, found)
    return found


def kernel(
    tok_ref, route_ref, rw_ref, w_hbm, out_ref, amax_ref,
    w_ref, wt, st, dt, tb, rz, ry, tx, xf, mt, mz, ms, my, mf,
    am_rows, am_send, am_z, am_y, am_x, am_c,
    pf, pa, xa, rl, sl, rs, ss, qb, xb, ysa, ysb, ya, yb,
    w_sem, s_tz, r_tz, s_mz, r_mz, s_ty, r_ty, s_my, r_my, s_tx, r_tx, s_mx, r_mx, s_tc, r_tc, s_mc, r_mc,
    s_az, r_az, s_ay, r_ay, s_ax, r_ax, s_ac, r_ac,
    s_xa, r_xa, s_rl, r_rl, s_rs, r_rs, s_xb, r_xb, s_ya, r_ya, s_yb, r_yb,
):
    e = lax.axis_index("expert")
    t = lax.axis_index("tensor")
    x = lax.rem(e, NX)
    z = lax.rem(e // NX, NZ)
    y = e // (NX * NZ)
    core = lax.rem(t, 2)
    low = t // 2

    def at(yy, zz, xx):
        return (yy * NZ + zz) * NX + xx

    def zp(o):
        return (at(y, lax.rem(z + o, NZ), x), t)

    def yp(o):
        return (at(lax.rem(y + o, NY), z, x), t)

    def xp(o):
        return (at(y, z, lax.rem(x + o, NX)), t)

    sibling = (e, low * 2 + (1 - core))
    across = (e, (1 - low) * 2 + core)

    def remote(src, dst, ssem, rsem, device):
        return pltpu.make_async_remote_copy(
            src_ref=src, dst_ref=dst, send_sem=ssem, recv_sem=rsem, device_id=device, device_id_type=MESH
        )

    load_w = pltpu.make_async_copy(w_hbm, w_ref, w_sem)
    load_w.start()

    barrier = pltpu.get_barrier_semaphore()
    peers = [zp(o) for o in range(1, NZ)] + [yp(o) for o in range(1, NY)] + [xp(o) for o in range(1, NX)]
    peers += [sibling, across]
    for device in peers:
        pl.semaphore_signal(barrier, inc=1, device_id=device, device_id_type=MESH)

    rows = pl.ds(pl.multiple_of(core * HALF, HALF), HALF)
    for zz in range(NZ):
        for yy in range(NY):
            tb[zz, yy] = tok_ref[rows, (yy * NZ + zz) * LANES:(yy * NZ + zz + 1) * LANES]
    place = (
        lax.broadcasted_iota(jnp.int32, (2 * HALF, LANES), 1)
        == lax.broadcasted_iota(jnp.int32, (2 * HALF, LANES), 0) + (z - core) * HALF
    ) & (lax.broadcasted_iota(jnp.int32, (2 * HALF, LANES), 1) // HALF == z)
    place = place.astype(F32)
    mt[0:TOP] = jnp.dot(route_ref[...].astype(F32), place, precision=lax.Precision.HIGHEST, preferred_element_type=F32)
    mt[TOP:2 * TOP] = jnp.dot(rw_ref[...], place, precision=lax.Precision.HIGHEST, preferred_element_type=F32)
    pl.semaphore_wait(barrier, len(peers))

    def tz(o):
        return remote(tb.at[lax.rem(z + o, NZ)], rz.at[z], s_tz.at[o - 1], r_tz.at[o - 1], zp(o))

    def tz_in(o):
        return remote(tb.at[z], rz.at[lax.rem(z + NZ - o, NZ)], s_tz.at[o - 1], r_tz.at[o - 1], zp(o))

    def mzc(o):
        return remote(mt, mz.at[o - 1], s_mz.at[o - 1], r_mz.at[o - 1], zp(o))

    def tyc(oy, o):
        zs = lax.rem(z + NZ - o, NZ)
        src = (rz if o else tb).at[zs, lax.rem(y + oy, NY)]
        return remote(src, ry.at[y, zs], s_ty.at[oy - 1, o], r_ty.at[oy - 1, o], yp(oy))

    def ty_in(oy, o):
        zs = lax.rem(z + NZ - o, NZ)
        return remote(tb.at[z, y], ry.at[lax.rem(y + NY - oy, NY), zs], s_ty.at[oy - 1, o], r_ty.at[oy - 1, o], yp(oy))

    def myc(o):
        return remote(ms, my.at[y], s_my.at[o - 1], r_my.at[o - 1], yp(o))

    def my_in(o):
        return remote(ms, my.at[lax.rem(y + NY - o, NY)], s_my.at[o - 1], r_my.at[o - 1], yp(o))

    def mxc(ox, oy):
        ys = lax.rem(y + NY - oy, NY)
        return remote(my.at[ys], mf.at[core, x, ys], s_mx.at[ox - 1, oy], r_mx.at[ox - 1, oy], xp(ox))

    def mx_in(ox, oy):
        ys = lax.rem(y + NY - oy, NY)
        dst = mf.at[core, lax.rem(x + NX - ox, NX), ys]
        return remote(my.at[ys], dst, s_mx.at[ox - 1, oy], r_mx.at[ox - 1, oy], xp(ox))

    def txc(ox, oy):
        ys = lax.rem(y + NY - oy, NY)
        src = tx.at[lax.rem(x + ox, NX), ys]
        return remote(src, xf.at[core, x, ys], s_tx.at[ox - 1, oy], r_tx.at[ox - 1, oy], xp(ox))

    def tx_in(ox, oy):
        ys = lax.rem(y + NY - oy, NY)
        dst = xf.at[core, lax.rem(x + NX - ox, NX), ys]
        return remote(tx.at[x, ys], dst, s_tx.at[ox - 1, oy], r_tx.at[ox - 1, oy], xp(ox))

    def mcc(ox, h):
        part = mf.at[h, lax.rem(x + NX - ox, NX)]
        return remote(part, part, s_mc.at[ox], r_mc.at[ox], sibling)

    def tcc(ox, h):
        part = xf.at[h, lax.rem(x + NX - ox, NX)]
        return remote(part, part, s_tc.at[ox], r_tc.at[ox], sibling)

    for o in (4, 3, 5, 2, 6, 1, 7):
        mzc(o).start()
        tz(o).start()
    for oy in (2, 1, 3):
        tyc(oy, 0).start()
    ry[y, z] = tb[z, y]

    load_w.wait()

    def turn_w(i, _):
        r = pl.multiple_of(i * 256, 256)
        block = w_ref[pl.ds(r, 256), :]
        wt[:, pl.ds(r, 256)] = block.T
        big = jnp.abs(block)
        big = jnp.maximum(jnp.maximum(big[:, 0:128], big[:, 128:256]), big[:, 256:384])
        am_rows[pl.ds(pl.multiple_of(i * 8, 8), 8), :] = jnp.max(big.astype(F32).reshape(8, DEPTH, LANES), axis=1)
        return 0

    lax.fori_loop(0, 16, turn_w, 0)
    am_send[0] = jnp.max(am_rows[...].T.reshape(16, 8, LANES), axis=0)

    gathered = mt[...]
    for o in (1, 7, 2, 6, 3, 5, 4):
        tz_in(o).wait_recv()
        for oy in (2, 1, 3):
            tyc(oy, o).start()
        zs = lax.rem(z + NZ - o, NZ)
        ry[y, zs] = rz[zs, y]
        mzc(o).wait_recv()
        gathered = gathered + mz[o - 1]
    ms[...] = gathered
    my[y] = gathered
    for o in (2, 1, 3):
        myc(o).start()

    for oy in (0, 1, 3, 2):
        ys = lax.rem(y + NY - oy, NY)
        if oy:
            my_in(oy).wait_recv()
            for o in range(NZ):
                ty_in(oy, o).wait_recv()
        for ox in (2, 1, 3):
            mxc(ox, oy).start()
        mf[core, x, ys] = my[ys]
        turned = ry[ys].reshape(NZ * HALF, LANES).T
        for xx in range(NX):
            tx[xx, ys] = turned[xx * DEPTH:(xx + 1) * DEPTH, :]
        for ox in (2, 1, 3):
            txc(ox, oy).start()
        xf[core, x, ys] = tx[x, ys]
    mcc(0, core).start()
    tcc(0, core).start()

    def x_arrived():
        for ox in (1, 3, 2):
            for oy in range(NY):
                mx_in(ox, oy).wait_recv()
                tx_in(ox, oy).wait_recv()
            mcc(ox, core).start()
            tcc(ox, core).start()

    def core_arrived():
        for ox in range(NX):
            mcc(ox, 1 - core).wait_recv()
            tcc(ox, 1 - core).wait_recv()

    def compute(i):
        h = lax.rem(core + pick(i, [half for half, _ in ORDER]), 2)
        xx = lax.rem(x + pick(i, [off for _, off in ORDER]), NX)
        ids = lax.broadcasted_iota(jnp.int32, (EXPERTS, LANES), 0).astype(F32)
        for yy in range(NY):
            dense = jnp.zeros((EXPERTS, LANES), F32)
            meta = mf[h, xx, yy]
            for k in range(TOP):
                dense = jnp.where(ids == meta[k:k + 1, :], meta[TOP + k:TOP + k + 1, :], dense)
            dt[:, yy * LANES:(yy + 1) * LANES] = dense
        features = jnp.concatenate([xf[h, xx, yy] for yy in range(NY)], axis=1).astype(F32)

        for n in range(EXPERTS):
            st[n * DEPTH:(n + 1) * DEPTH, :] = (features * dt[n:n + 1, :]).astype(BF)
        part = jnp.dot(wt[...], st[...], preferred_element_type=F32).T
        for yy in range(NY):
            for zz in range(NZ):
                r = (yy * NZ + zz) * HALF
                pf[i, zz, yy] = part[r:r + HALF, :]

    ways = (-1, -1, 1, 1)

    def xac(half, off, p):
        k = 2 * half + SENT[off]
        part = pl.ds(4 * p, 4)
        return remote(pa.at[k, part], xa.at[k, part], s_xa.at[k, p], r_xa.at[k, p], xp(off))

    def held_block(j, rel):
        half = j % 2
        block = pf[ORDER.index((half, 2 if j < 2 else 0)), lax.rem(z + rel, NZ)]
        if j < 2:
            return block
        r = FAR_FIRST.index(rel)
        return block + xa[2 * half, r].astype(F32) + xa[2 * half + 1, r].astype(F32)

    def ring_long(j, s):
        return remote(sl.at[j, s - 1], rl.at[j, s - 1], s_rl.at[j, s - 1], r_rl.at[j, s - 1], zp(NZ + ways[j]))

    def ring_short(j, s):
        return remote(ss.at[j, s - 1], rs.at[j, s - 1], s_rs.at[j, s - 1], r_rs.at[j, s - 1], zp(NZ - ways[j]))

    def xbc(half):
        return remote(qb.at[half], xb.at[half], s_xb.at[half], r_xb.at[half], xp(2))

    def ring_step(j, s):
        if j >= 2 and s in (1, 3):
            for off in SENT:
                xac(j % 2, off, s // 2).wait_recv()
        block = held_block(j, (ways[j] * (5 - s)) % NZ)
        if s > 1:
            ring_long(j, s - 1).wait_recv()
            block = block + rl[j, s - 2].astype(F32)
        sl[j, s - 1] = block.astype(BF)
        ring_long(j, s).start()
        if s < 4:
            block = held_block(j, (-ways[j] * (4 - s)) % NZ)
            if s > 1:
                ring_short(j, s - 1).wait_recv()
                block = block + rs[j, s - 2].astype(F32)
            ss[j, s - 1] = block.astype(BF)
            ring_short(j, s).start()

    def yac(o):
        return remote(ysa.at[lax.rem(y + o, NY)], ya.at[o - 1], s_ya.at[o - 1], r_ya.at[o - 1], yp(o))

    def ybc(o):
        return remote(ysb.at[lax.rem(y + o, NY)], yb.at[o - 1], s_yb.at[o - 1], r_yb.at[o - 1], yp(o))

    def ring_end(j):
        ring_long(j, 4).wait_recv()
        ring_short(j, 3).wait_recv()
        qb[j] = held_block(j, 0) + rl[j, 3].astype(F32) + rs[j, 2].astype(F32)
        if j < 2:
            xbc(j).start()
            return
        kept, copies = ((ysa, yac), (ysb, ybc))[j - 2]
        xbc(j - 2).wait_recv()
        kept[...] = qb[j] + xb[j - 2]
        for o in (2, 1, 3):
            copies(o).start()

    def azc(o):
        return remote(am_send.at[0], am_z.at[o - 1], s_az.at[o - 1], r_az.at[o - 1], zp(o))

    def ayc(o):
        return remote(am_send.at[1], am_y.at[o - 1], s_ay.at[o - 1], r_ay.at[o - 1], yp(o))

    def axc(o):
        return remote(am_send.at[2], am_x.at[o - 1], s_ax.at[o - 1], r_ax.at[o - 1], xp(o))

    def acc(k):
        return remote(am_send.at[3 + k], am_c.at[k], s_ac.at[k], r_ac.at[k], sibling if k == 0 else across)

    def amax_stage(n):
        top = am_send[n - 1] if n else None
        for o in range(1, NZ) if n == 1 else range(1, NY) if n == 2 else range(1, NX) if n == 3 else ():
            (azc, ayc, axc)[n - 1](o).wait_recv()
            top = jnp.maximum(top, (am_z, am_y, am_x)[n - 1][o - 1])
        if n == 4:
            acc(0).wait_recv()
            top = jnp.maximum(top, am_c[0])
        if n:
            am_send[n] = top
        if n < 3:
            for o in range(1, (NZ, NY, NX)[n]):
                (azc, ayc, axc)[n](o).start()
        else:
            acc(n - 3).start()

    def after(i):
        if i < 8 and ORDER[i][1] in SENT:
            half, off = ORDER[i]
            for r, rel in enumerate(FAR_FIRST):
                pa[2 * half + SENT[off], r] = pf[i, lax.rem(z + rel, NZ)].astype(BF)
                if r == 3:
                    xac(half, off, 0).start()
        for half in range(2):
            if i == SECOND[half]:
                for off in SENT:
                    xac(half, off, 1).start()
        for s in (1, 0, 5, 4, 3, 2):
            if s == 0 and i == 0:
                x_arrived()
            for j, when in enumerate(RINGS):
                if s and when[s - 1] == i:
                    ring_end(j) if s == 5 else ring_step(j, s)
        if i in AMAX:
            amax_stage(AMAX.index(i))

    def step(i, _):
        @pl.when(i == 2)
        def _():
            core_arrived()

        @pl.when(i < 8)
        def _():
            compute(i)

        for n in range(STEPS):
            pl.when(i == n)(lambda n=n: after(n))
        return 0

    lax.fori_loop(0, STEPS, step, 0)

    acc(1).wait_recv()
    top = jnp.max(jnp.maximum(am_send[4], am_c[1]), axis=0, keepdims=True)
    mine = lax.broadcasted_iota(jnp.int32, (1, LANES), 1) == e
    amax_ref[0] = jnp.max(jnp.where(mine, top, 0.0))

    for source, copies, arrived, other in ((ysa, yac, ya, 0), (ysb, ybc, yb, 1)):
        total = source[y]
        for o in range(1, NY):
            copies(o).wait_recv()
            total = total + arrived[o - 1]
        half = lax.rem(core + other, 2)
        out_ref[pl.ds(pl.multiple_of(half * HALF, HALF), HALF), :] = total.astype(BF)

    for o in range(1, NZ):
        tz(o).wait_send()
        mzc(o).wait_send()
        azc(o).wait_send()
    for oy in range(1, NY):
        for o in range(NZ):
            tyc(oy, o).wait_send()
        myc(oy).wait_send()
        ayc(oy).wait_send()
        yac(oy).wait_send()
        ybc(oy).wait_send()
    for ox in range(1, NX):
        for oy in range(NY):
            txc(ox, oy).wait_send()
            mxc(ox, oy).wait_send()
        axc(ox).wait_send()
    for ox in range(NX):
        mcc(ox, core).wait_send()
        tcc(ox, core).wait_send()
    for k in range(2):
        acc(k).wait_send()
        xbc(k).wait_send()
        for off in SENT:
            xac(k, off, 0).wait_send()
            xac(k, off, 1).wait_send()
    for j in range(4):
        for s in range(1, 5):
            ring_long(j, s).wait_send()
            if s < 4:
                ring_short(j, s).wait_send()


def shards(tokens, routes, route_weights, learner_weights):
    vmem = pl.BlockSpec(memory_space=pltpu.VMEM)
    block = (NY, HALF, WIDTH)

    def dma(*shape):
        return [pltpu.SemaphoreType.DMA(shape), pltpu.SemaphoreType.DMA(shape)]

    combined, amax = pl.pallas_call(
        kernel,
        out_shape=(
            jax.ShapeDtypeStruct((2 * HALF, WIDTH), BF),
            jax.ShapeDtypeStruct((1,), F32),
        ),
        in_specs=[vmem, vmem, vmem, pl.BlockSpec(memory_space=pl.ANY)],
        out_specs=(vmem, pl.BlockSpec(memory_space=pltpu.SMEM)),
        scratch_shapes=[
            pltpu.VMEM((EXPERTS * DEPTH, WIDTH), BF),
            pltpu.VMEM((WIDTH, EXPERTS * DEPTH), BF),
            pltpu.VMEM((EXPERTS * DEPTH, COLS), BF),
            pltpu.VMEM((EXPERTS, COLS), F32),
            pltpu.VMEM((NZ, NY, HALF, LANES), BF),
            pltpu.VMEM((NZ, NY, HALF, LANES), BF),
            pltpu.VMEM((NY, NZ, HALF, LANES), BF),
            pltpu.VMEM((NX, NY, DEPTH, LANES), BF),
            pltpu.VMEM((2, NX, NY, DEPTH, LANES), BF),
            pltpu.VMEM((2 * TOP, LANES), F32),
            pltpu.VMEM((NZ - 1, 2 * TOP, LANES), F32),
            pltpu.VMEM((2 * TOP, LANES), F32),
            pltpu.VMEM((NY, 2 * TOP, LANES), F32),
            pltpu.VMEM((2, NX, NY, 2 * TOP, LANES), F32),
            pltpu.VMEM((EXPERTS, LANES), F32),
            pltpu.VMEM((5, 8, LANES), F32),
            pltpu.VMEM((NZ - 1, 8, LANES), F32),
            pltpu.VMEM((NY - 1, 8, LANES), F32),
            pltpu.VMEM((NX - 1, 8, LANES), F32),
            pltpu.VMEM((2, 8, LANES), F32),
            pltpu.VMEM((8, NZ, *block), F32),
            pltpu.VMEM((4, NZ, *block), BF),
            pltpu.VMEM((4, NZ, *block), BF),
            pltpu.VMEM((4, 4, *block), BF),
            pltpu.VMEM((4, 4, *block), BF),
            pltpu.VMEM((4, 3, *block), BF),
            pltpu.VMEM((4, 3, *block), BF),
            pltpu.VMEM((4, *block), F32),
            pltpu.VMEM((2, *block), F32),
            pltpu.VMEM(block, F32),
            pltpu.VMEM(block, F32),
            pltpu.VMEM((NY - 1, HALF, WIDTH), F32),
            pltpu.VMEM((NY - 1, HALF, WIDTH), F32),
            pltpu.SemaphoreType.DMA,
            *dma(NZ - 1), *dma(NZ - 1), *dma(NY - 1, NZ), *dma(NY - 1), *dma(NX - 1, NY), *dma(NX - 1, NY), *dma(NX), *dma(NX),
            *dma(NZ - 1), *dma(NY - 1), *dma(NX - 1), *dma(2),
            *dma(4, 2), *dma(4, 4), *dma(4, 3), *dma(2), *dma(NY - 1), *dma(NY - 1),
        ],
        compiler_params=pltpu.CompilerParams(
            collective_id=0, has_side_effects=True, vmem_limit_bytes=60 * 2**20
        ),
        name="relay",
    )(tokens, routes.T, route_weights.T, learner_weights.reshape(EXPERTS * DEPTH, WIDTH))
    return combined, amax


def solution(mesh):
    return jax.shard_map(
        shards,
        mesh=mesh,
        in_specs=(
            P("expert", None),
            P("expert", None),
            P("expert", None),
            P(None, "expert", "tensor"),
        ),
        out_specs=(P("expert", "tensor"), P("expert")),
        check_vma=False,
    )
```
